32 devices in a mesh: dp: 8 (over z, y), tensor: 4 (over x, core).
Axes of the slice: x: 2, y: 2, z: 4, core: 2. Of those that a mesh axis runs over, the one named last changes fastest.
Arguments:
- block_in: bfloat16 [4096, 2048], P(('dp', 'tensor')), may hold values from -6 to 6
- cotangent: bfloat16 [4096, 2048], P(('dp', 'tensor')), may hold values from -6 to 6
- segments: int32 [4096], P('dp'), may hold values from 0 to 31, never falling along the last dimension, each value on 1 to 512 neighbouring positions
- expert_ids: int32 [4096, 8], P(('dp', 'tensor')), may hold values from 0 to 15, all different within a row; in each aligned block of 128 rows (0 to 127, 128 to 255, ...) at most 96 rows name the same one
- attn_gain: bfloat16 [2048], P('dp'), may hold values from 0.25 to 1.75
- w_query: bfloat16 [2048, 2048], P('dp', 'tensor'), may hold values from -0.125 to 0.125
- w_key: bfloat16 [2048, 2048], P('dp', 'tensor'), may hold values from -0.125 to 0.125
- w_value: bfloat16 [2048, 2048], P('dp', 'tensor'), may hold values from -0.125 to 0.125
- query_gain: bfloat16 [16, 128], P('tensor', 'dp'), may hold values from 0.25 to 1.75
- key_gain: bfloat16 [16, 128], P('tensor', 'dp'), may hold values from 0.25 to 1.75
- w_out: bfloat16 [2048, 2048], P('tensor', 'dp'), may hold values from -1 to 1
- ffn_gain: bfloat16 [2048], P('dp'), may hold values from 0.25 to 1.75
- router: bfloat16 [2048, 16], P('dp'), may hold values from -0.125 to 0.125
- w_gate: bfloat16 [16, 2048, 1024], P('dp', None, 'tensor'), may hold values from -0.125 to 0.125
- w_up: bfloat16 [16, 2048, 1024], P('dp', None, 'tensor'), may hold values from -0.125 to 0.125
- w_down: bfloat16 [16, 1024, 2048], P('dp', 'tensor'), may hold values from -4 to 4
Outputs:
- block_out: bfloat16 [4096, 2048], P(('dp', 'tensor'))
- d_block_in: float32 [4096, 2048], P(('dp', 'tensor'))
- d_attn_gain: float32 [2048], P(('dp', 'tensor'))
- d_w_query: float32 [2048, 2048], P('dp', 'tensor')
- d_w_key: float32 [2048, 2048], P('dp', 'tensor')
- d_w_value: float32 [2048, 2048], P('dp', 'tensor')
- d_query_gain: float32 [16, 128], P('tensor', 'dp')
- d_key_gain: float32 [16, 128], P('tensor', 'dp')
- d_w_out: float32 [2048, 2048], P('tensor', 'dp')
- d_ffn_gain: float32 [2048], P(('dp', 'tensor'))
- d_router: float32 [2048, 16], P(('dp', 'tensor'))
- d_w_gate: float32 [16, 2048, 1024], P('dp', None, 'tensor')
- d_w_up: float32 [16, 2048, 1024], P('dp', None, 'tensor')
- d_w_down: float32 [16, 1024, 2048], P('dp', 'tensor')
The draws below stay inside these ranges and needn't reach their ends.
Inputs may be any that keep to these rules, and one draw needn't show every extreme that they name: `expert_ids`: each row names 8 different experts. In each aligned block of 128 rows (the rows of one device), no expert is named by more than 96 rows, a bound that some block reaches. `segments`: never falling along the tokens; every document has 1 to 512 tokens and one has exactly 512.
All inputs are finite; a program needn't handle non-finite values.
Results may differ from the reference program's by a relative error of at most 0.025.
Values may be sent and summed in bfloat16 or wider, within the bound.
No kernel may reach another device: no remote copies, remote signals or barrier semaphores. Data moves between devices by JAX's collectives and lax.ppermute only.
A program may use at most 384 MiB of HBM per device.

```python
import math
import jax
import jax.numpy as jnp
import numpy as np
from jax import lax

D = 2048
HEADS = 16
HD = 128
FF = 1024
TOPK = 8
SEQ = 512
E = 16
QTOK = 128
TOKENS = 4096
CAP = 96


def shard_levels(key, shape, split, least, high):
    loudness = 1.0
    for dim, shards_of in split:
        heights = jax.random.uniform(jax.random.fold_in(jax.random.fold_in(key, 6), dim), (shards_of,), jnp.float32, least / len(split), high / len(split))
        loudness = loudness * jnp.repeat(jnp.exp(heights), shape[dim] // shards_of).reshape((-1,) + (1,) * (len(shape) - 1 - dim))
    return loudness


def split_up(amount, total, most, skew):
    portions = [(1 << 20) // math.isqrt(grade ** skew) + 1 for grade in range(2, amount + 1)]
    rest, given = total - most - (amount - 1), [1] * (amount - 1)
    while rest > 0:
        free = [i for i in range(amount - 1) if given[i] < most]
        whole, budget = sum([portions[i] for i in free]), rest
        for i in free:
            addition = min(most - given[i], max(1, budget * portions[i] // whole), rest)
            given[i] = given[i] + addition
            rest = rest - addition
    return np.array([most] + given)


def uneven(rng, count, total, bound, skew):
    if count == 2:
        one = jax.random.randint(rng, (), max(1, total - bound), min(bound, total - 1) + 1)
        return jnp.stack([one, total - one])
    tallies = jnp.asarray(split_up(count, total, bound, skew), jnp.int32)
    couples = (count - 1) // 2
    donor, taker = tallies[1:1 + 2 * couples:2], tallies[2:2 + 2 * couples:2]
    slack = jnp.minimum(donor - 1, bound - taker)
    moved = jax.random.randint(jax.random.fold_in(rng, 1), (couples,), 0, 1 << 20) % (slack + 1)
    tallies = tallies.at[1:1 + 2 * couples:2].set(donor - moved).at[2:2 + 2 * couples:2].set(taker + moved)
    return tallies[jax.random.permutation(jax.random.fold_in(rng, 2), count)]


def shared_out(rng, own, number, rows, number_of, top, bound, skew):
    sequence = jax.random.permutation(rng, number_of)
    crowded, ordinary = load_shares(number_of, rows * top, bound, skew, True), load_shares(number_of, rows * top, bound, skew, False)
    places = jnp.arange(number_of)

    def named(lengths, rotation):
        used = int((lengths > 0).sum())
        fixed = max(1, used // 4)
        moved = fixed + (places - fixed + rotation * (used - fixed)) % max(1, number_of - fixed)
        return jnp.zeros((number_of,), jnp.int32).at[sequence[jnp.where(places < fixed, places, moved)]].set(jnp.asarray(lengths, jnp.int32))

    lengths = jnp.where(number % 4 == 0, named(crowded, number // 4), named(ordinary, number - number // 4 - 1))
    mixed = jax.random.permutation(jax.random.fold_in(own, 3), number_of)
    source_of, receiver = mixed[0:number_of // 2 * 2:2], mixed[1:number_of // 2 * 2:2]
    slack = jnp.minimum(lengths[source_of] - 1, bound - lengths[receiver]) // 2
    slack = jnp.where((source_of == sequence[0]) | (receiver == sequence[0]) | (lengths[receiver] == 0), 0, jnp.maximum(slack, 0))
    moved = jax.random.randint(jax.random.fold_in(own, 4), (number_of // 2,), 0, 1 << 20) % (slack + 1)
    lengths = lengths.at[source_of].add(-moved).at[receiver].add(moved)
    items = jnp.searchsorted(jnp.cumsum(lengths), jnp.arange(rows * top), side="right").astype(jnp.int32)
    grid = items.reshape(top, rows).T
    grid = grid[jax.random.permutation(jax.random.fold_in(own, 1), rows)]
    rotation = jax.random.randint(jax.random.fold_in(own, 2), (rows, 1), 0, top)
    return jnp.take_along_axis(grid, (jnp.arange(top)[None, :] + rotation) % top, axis=1)


def load_shares(amount, total, most, skew, full):
    loads = [(1 << 20) // math.isqrt(grade ** skew) + 1 for grade in range(1, amount + 1)]
    largest = most if full else min(most, max(-(-total // amount), total * loads[0] // sum(loads)))
    least = 1 if total - largest >= amount - 1 else 0
    holding, rest = [largest] + [least] * (amount - 1), total - largest - least * (amount - 1)
    while rest > 0:
        movable = [i for i in range(1, amount) if holding[i] < largest] or [i for i in range(1, amount) if holding[i] < most]
        whole, remaining = sum([loads[i] for i in movable]), rest
        for i in movable:
            more = min(most - holding[i], max(1, remaining * loads[i] // whole), rest)
            holding[i] = holding[i] + more
            rest = rest - more
    return np.array(holding)


def bell_draw(key, extent, scale, reach, pieces=(), held_as=jnp.bfloat16):
    entries = jax.random.normal(key, extent, jnp.float32) * scale
    if len(pieces) > 0:
        entries = shard_levels(key, extent, pieces, -0.22, 0.18) * entries
    return jnp.clip(entries, min=-reach, max=reach).astype(held_as)


def setup_inputs(seed: int = 0) -> dict:
    seeds = jax.random.split(jax.random.key(seed), 17)
    block_in = bell_draw(seeds[0], (TOKENS, D), 1.0, 6.0, ((0, 32),))
    cotangent = bell_draw(seeds[1], (TOKENS, D), 1.0, 6.0, ((0, 32),))
    segments = jnp.searchsorted(jnp.cumsum(uneven(seeds[2], TOKENS // (SEQ // 4), TOKENS, SEQ, 2)), jnp.arange(TOKENS), side="right").astype(jnp.int32)
    expert_ids_keys = jax.random.split(jax.random.fold_in(seeds[3], 1), TOKENS // QTOK)
    expert_ids_turns = jax.random.permutation(jax.random.fold_in(seeds[3], 3), TOKENS // QTOK)
    expert_ids = jax.vmap(lambda own, number: shared_out(jax.random.fold_in(seeds[3], 2), own, number, QTOK, E, TOPK, CAP, 1))(expert_ids_keys, expert_ids_turns).reshape((TOKENS, TOPK))
    attn_gain = jnp.clip(1.0 + 0.15 * jax.random.normal(seeds[4], (D,), jnp.float32), 0.25, 1.75).astype(jnp.bfloat16)
    w_query = bell_draw(seeds[5], (D, D), D ** -0.5, 0.125, ((0, 8), (1, 4)))
    w_key = bell_draw(seeds[6], (D, D), D ** -0.5, 0.125, ((0, 8), (1, 4)))
    w_value = bell_draw(seeds[7], (D, D), D ** -0.5, 0.125, ((0, 8), (1, 4)))
    query_gain = jnp.clip(1.0 + 0.15 * jax.random.normal(seeds[8], (HEADS, HD), jnp.float32), 0.25, 1.75).astype(jnp.bfloat16)
    key_gain = jnp.clip(1.0 + 0.15 * jax.random.normal(seeds[9], (HEADS, HD), jnp.float32), 0.25, 1.75).astype(jnp.bfloat16)
    w_out = bell_draw(seeds[10], (D, D), (D // 64) ** -0.5, 1.0, ((0, 4), (1, 8)))
    ffn_gain = jnp.clip(1.0 + 0.15 * jax.random.normal(seeds[11], (D,), jnp.float32), 0.25, 1.75).astype(jnp.bfloat16)
    router = bell_draw(seeds[12], (D, E), D ** -0.5, 0.125, ((0, 8),))
    w_gate = bell_draw(seeds[13], (E, D, FF), D ** -0.5, 0.125, ((0, 8), (2, 4)))
    w_up = bell_draw(seeds[14], (E, D, FF), D ** -0.5, 0.125, ((0, 8), (2, 4)))
    w_down = bell_draw(seeds[15], (E, FF, D), (max(1, FF // 512)) ** -0.5, 4.0, ((0, 8), (1, 4)))
    return dict(block_in=block_in, cotangent=cotangent, segments=segments, expert_ids=expert_ids, attn_gain=attn_gain, w_query=w_query, w_key=w_key, w_value=w_value, query_gain=query_gain, key_gain=key_gain, w_out=w_out, ffn_gain=ffn_gain, router=router, w_gate=w_gate, w_up=w_up, w_down=w_down)


EPS = 1e-05

def rstd_of(values):
    return lax.rsqrt(lax.optimization_barrier(jnp.mean(values * values, axis=-1, keepdims=True)) + EPS)

def rope_tables(count, head_size):
    positions = (jnp.arange(count) % SEQ).astype(jnp.float32)
    half = head_size // 2
    freq = 10000.0 ** (-(jnp.arange(half).astype(jnp.float32) * 2.0 / head_size))
    angle = positions[:, None] * freq[None, :]
    return (jnp.cos(angle), jnp.sin(angle))

def rotate(values, cosine, sine):
    half = values.shape[-1] // 2
    first, second = (values[..., :half], values[..., half:])
    c_tab = cosine[:, None, :]
    s_tab = sine[:, None, :]
    return jnp.concatenate([first * c_tab - second * s_tab, second * c_tab + first * s_tab], axis=-1)

def unrotate(values, cosine, sine):
    half = values.shape[-1] // 2
    first, second = (values[..., :half], values[..., half:])
    c_tab = cosine[:, None, :]
    s_tab = sine[:, None, :]
    return jnp.concatenate([first * c_tab + second * s_tab, second * c_tab - first * s_tab], axis=-1)

def masked_scores(query, keys, segs, scale):
    scores = jnp.einsum('qhd,khd->hqk', query.astype(jnp.float32), keys.astype(jnp.float32)) * scale
    length = query.shape[0]
    causal = jnp.arange(length)[:, None] >= jnp.arange(length)[None, :]
    same = segs[:, None] == segs[None, :]
    return jnp.where((causal & same)[None], scores, -jnp.inf)

def slot_table(expert_ids):
    blocks = TOKENS // QTOK
    each = QTOK * TOPK
    flat_ids = expert_ids.reshape(blocks, each).astype(jnp.int32)
    onehot = (flat_ids[:, :, None] == jnp.arange(E).astype(jnp.int32)[None, None, :]).astype(jnp.int32)
    before = jnp.cumsum(onehot, axis=1) - onehot
    position = lax.optimization_barrier(jnp.sum(before * onehot, axis=2)).astype(jnp.int32)
    block_idx = jnp.arange(blocks).astype(jnp.int32)[:, None]
    target = ((flat_ids * blocks + block_idx) * CAP + position).astype(jnp.int32)
    assign = (block_idx * each + jnp.arange(each).astype(jnp.int32)[None, :]).astype(jnp.int32)
    table = jnp.full((E * blocks * CAP,), TOKENS * TOPK, jnp.int32)
    table = table.at[target.reshape(-1)].set(assign.reshape(-1))
    return table.reshape(E, blocks * CAP)

def reference(block_in, cotangent, segments, expert_ids, attn_gain, w_query, w_key, w_value, query_gain, key_gain, w_out, ffn_gain, router, w_gate, w_up, w_down):
    fp = jnp.float32
    low = jnp.bfloat16
    in_full = block_in.astype(fp)
    r_one = rstd_of(in_full)
    n_one = in_full * r_one
    attn_g = attn_gain.astype(fp)
    h_one = (n_one * attn_g).astype(low)
    q_raw = jnp.dot(h_one, w_query, preferred_element_type=fp)
    k_raw = jnp.dot(h_one, w_key, preferred_element_type=fp)
    value = jnp.dot(h_one, w_value, preferred_element_type=fp).astype(low)
    r_q = rstd_of(q_raw)
    r_k = rstd_of(k_raw)
    q_gainf = query_gain.reshape(-1).astype(fp)
    k_gainf = key_gain.reshape(-1).astype(fp)
    cosine, sine = rope_tables(TOKENS, HD)
    q_rot = rotate((q_raw * r_q * q_gainf).reshape(TOKENS, HEADS, HD), cosine, sine).astype(low)
    k_rot = rotate((k_raw * r_k * k_gainf).reshape(TOKENS, HEADS, HD), cosine, sine).astype(low)
    value_heads = value.reshape(TOKENS, HEADS, HD)
    scale = HD ** (-0.5)
    seqs = TOKENS // SEQ

    def by_sequence(arr):
        return arr.reshape((seqs, SEQ) + arr.shape[1:])

    def seq_forward(item):
        query, keys, values, segs = item
        masked = masked_scores(query, keys, segs, scale)
        top = lax.optimization_barrier(jnp.max(masked, axis=-1, keepdims=True))
        lse = top + jnp.log(lax.optimization_barrier(jnp.sum(jnp.exp(masked - top), axis=-1, keepdims=True)))
        prob = jnp.exp(masked - lse).astype(low)
        heads_out = jnp.einsum('hqk,khd->qhd', prob.astype(fp), values.astype(fp)).astype(low)
        return (heads_out, lse)
    seq_items = (by_sequence(q_rot), by_sequence(k_rot), by_sequence(value_heads), by_sequence(segments))
    attn_heads, lse_all = lax.map(seq_forward, seq_items)
    attn_heads = attn_heads.reshape(TOKENS, D)
    resid = in_full + jnp.dot(attn_heads, w_out, preferred_element_type=fp)
    r_two = rstd_of(resid)
    n_two = resid * r_two
    ffn_g = ffn_gain.astype(fp)
    h_two = (n_two * ffn_g).astype(low)
    logits = jnp.dot(h_two, router, preferred_element_type=fp)
    probs = jax.nn.softmax(logits, axis=-1)
    weights = jnp.take_along_axis(probs, expert_ids, axis=1)
    table = slot_table(expert_ids)
    h_pad = jnp.concatenate([h_two, jnp.zeros((1, D), low)], axis=0)
    w_pad = jnp.concatenate([weights.reshape(-1), jnp.zeros((1,), fp)], axis=0)

    def expert_forward(acc, item):
        assign, gate_w, up_w, down_w = item
        rows = assign // TOPK
        inputs = h_pad[rows]
        gate = jnp.dot(inputs, gate_w, preferred_element_type=fp)
        up_val = jnp.dot(inputs, up_w, preferred_element_type=fp)
        act = (gate * jax.nn.sigmoid(gate) * up_val).astype(low)
        expert_out = jnp.dot(act, down_w, preferred_element_type=fp)
        return (acc.at[rows].add(w_pad[assign][:, None] * expert_out), None)
    moe_acc, _ = lax.scan(expert_forward, jnp.zeros((TOKENS + 1, D), fp), (table, w_gate, w_up, w_down))
    block_out = (resid + moe_acc[:TOKENS]).astype(low)
    g_full = cotangent.astype(fp)
    g_pad = jnp.concatenate([g_full, jnp.zeros((1, D), fp)], axis=0)

    def expert_backward(carry, item):
        d_h_acc, d_w_acc = carry
        assign, gate_w, up_w, down_w = item
        rows = assign // TOPK
        inputs = h_pad[rows]
        gate = jnp.dot(inputs, gate_w, preferred_element_type=fp)
        up_val = jnp.dot(inputs, up_w, preferred_element_type=fp)
        sig = jax.nn.sigmoid(gate)
        act = (gate * sig * up_val).astype(low)
        expert_out = jnp.dot(act, down_w, preferred_element_type=fp)
        g_rows = g_pad[rows]
        d_w_acc = d_w_acc.at[assign].add(lax.optimization_barrier(jnp.sum(g_rows * expert_out, axis=-1)))
        d_out = (w_pad[assign][:, None] * g_rows).astype(low)
        d_act = jnp.dot(d_out, down_w.T, preferred_element_type=fp)
        grad_down = jnp.dot(act.T, d_out, preferred_element_type=fp)
        d_gate = (d_act * up_val * sig * (1.0 + gate * (1.0 - sig))).astype(low)
        d_up = (d_act * gate * sig).astype(low)
        grad_gate = jnp.dot(inputs.T, d_gate, preferred_element_type=fp)
        grad_up = jnp.dot(inputs.T, d_up, preferred_element_type=fp)
        d_in = jnp.dot(d_gate, gate_w.T, preferred_element_type=fp) + jnp.dot(d_up, up_w.T, preferred_element_type=fp)
        d_h_acc = d_h_acc.at[rows].add(d_in)
        return ((d_h_acc, d_w_acc), (grad_gate, grad_up, grad_down))
    start = (jnp.zeros((TOKENS + 1, D), fp), jnp.zeros((TOKENS * TOPK + 1,), fp))
    (d_h_acc, d_w_acc), (d_w_gate, d_w_up, d_w_down) = lax.scan(expert_backward, start, (table, w_gate, w_up, w_down))
    d_weight = d_w_acc[:TOKENS * TOPK].reshape(TOKENS, TOPK)
    chosen = (expert_ids[:, :, None] == jnp.arange(E).astype(jnp.int32)[None, None, :]).astype(fp)
    d_probs = lax.optimization_barrier(jnp.sum(chosen * d_weight[:, :, None], axis=1))
    d_logits = (probs * (d_probs - lax.optimization_barrier(jnp.sum(probs * d_probs, axis=-1, keepdims=True)))).astype(low)
    d_router = jnp.dot(h_two.T, d_logits, preferred_element_type=fp)
    d_h_two = d_h_acc[:TOKENS] + jnp.dot(d_logits, router.T, preferred_element_type=fp)
    d_ffn_gain = lax.optimization_barrier(jnp.sum(d_h_two * n_two, axis=0))
    m_two = d_h_two * ffn_g
    d_resid = g_full + r_two * (m_two - n_two * lax.optimization_barrier(jnp.mean(m_two * n_two, axis=-1, keepdims=True)))
    d_resid_low = d_resid.astype(low)
    d_w_out = jnp.dot(attn_heads.T, d_resid_low, preferred_element_type=fp)
    d_heads = jnp.dot(d_resid_low, w_out.T, preferred_element_type=fp).astype(low).reshape(TOKENS, HEADS, HD)

    def seq_backward(item):
        query, keys, values, segs, lse, d_out = item
        masked = masked_scores(query, keys, segs, scale)
        prob = jnp.exp(masked - lse)
        prob_low = prob.astype(low).astype(fp)
        d_val = jnp.einsum('hqk,qhd->khd', prob_low, d_out.astype(fp))
        d_prob = jnp.einsum('qhd,khd->hqk', d_out.astype(fp), values.astype(fp))
        delta = lax.optimization_barrier(jnp.sum(prob * d_prob, axis=-1, keepdims=True))
        d_score = (prob * (d_prob - delta) * scale).astype(low).astype(fp)
        d_query = jnp.einsum('hqk,khd->qhd', d_score, keys.astype(fp))
        d_keys = jnp.einsum('hqk,qhd->khd', d_score, query.astype(fp))
        return (d_query, d_keys, d_val)
    back_items = seq_items + (lse_all, by_sequence(d_heads))
    d_q_rot, d_k_rot, d_value = lax.map(seq_backward, back_items)
    d_q_norm = unrotate(d_q_rot.reshape(TOKENS, HEADS, HD), cosine, sine).reshape(TOKENS, D)
    d_k_norm = unrotate(d_k_rot.reshape(TOKENS, HEADS, HD), cosine, sine).reshape(TOKENS, D)
    d_query_gain = lax.optimization_barrier(jnp.sum(d_q_norm * q_raw * r_q, axis=0)).reshape(HEADS, HD)
    d_key_gain = lax.optimization_barrier(jnp.sum(d_k_norm * k_raw * r_k, axis=0)).reshape(HEADS, HD)
    u_q = d_q_norm * q_gainf
    u_k = d_k_norm * k_gainf
    d_q_raw = (r_q * u_q - q_raw * r_q ** 3 * lax.optimization_barrier(jnp.mean(u_q * q_raw, axis=-1, keepdims=True))).astype(low)
    d_k_raw = (r_k * u_k - k_raw * r_k ** 3 * lax.optimization_barrier(jnp.mean(u_k * k_raw, axis=-1, keepdims=True))).astype(low)
    d_value_low = d_value.reshape(TOKENS, D).astype(low)
    d_w_query = jnp.dot(h_one.T, d_q_raw, preferred_element_type=fp)
    d_w_key = jnp.dot(h_one.T, d_k_raw, preferred_element_type=fp)
    d_w_value = jnp.dot(h_one.T, d_value_low, preferred_element_type=fp)
    d_h_one = jnp.dot(d_q_raw, w_query.T, preferred_element_type=fp)
    d_h_one = d_h_one + jnp.dot(d_k_raw, w_key.T, preferred_element_type=fp)
    d_h_one = d_h_one + jnp.dot(d_value_low, w_value.T, preferred_element_type=fp)
    d_attn_gain = lax.optimization_barrier(jnp.sum(d_h_one * n_one, axis=0))
    m_one = d_h_one * attn_g
    d_block_in = d_resid + r_one * (m_one - n_one * lax.optimization_barrier(jnp.mean(m_one * n_one, axis=-1, keepdims=True)))
    return (block_out, d_block_in, d_attn_gain, d_w_query, d_w_key, d_w_value, d_query_gain, d_key_gain, d_w_out, d_ffn_gain, d_router, d_w_gate, d_w_up, d_w_down)
```

```python
import jax
import jax.numpy as jnp
from jax import lax
from jax.sharding import PartitionSpec as P

SEQ = 512


EPS = 1e-05


def rstd_of(values):
    return lax.rsqrt(jnp.mean(values * values, axis=-1, keepdims=True) + EPS)


def rope_tables(count, head_size):
    positions = (jnp.arange(count) % SEQ).astype(jnp.float32)
    half = head_size // 2
    freq = 10000.0 ** (-(jnp.arange(half).astype(jnp.float32) * 2.0 / head_size))
    angle = positions[:, None] * freq[None, :]
    return (jnp.cos(angle), jnp.sin(angle))


def rotate(values, cosine, sine):
    half = values.shape[-1] // 2
    first, second = (values[..., :half], values[..., half:])
    c_tab = cosine[:, None, :]
    s_tab = sine[:, None, :]
    return jnp.concatenate(
        [first * c_tab - second * s_tab, second * c_tab + first * s_tab], axis=-1
    )


def unrotate(values, cosine, sine):
    half = values.shape[-1] // 2
    first, second = (values[..., :half], values[..., half:])
    c_tab = cosine[:, None, :]
    s_tab = sine[:, None, :]
    return jnp.concatenate(
        [first * c_tab + second * s_tab, second * c_tab - first * s_tab], axis=-1
    )


def masked_scores(query, keys, segs, scale):
    scores = jnp.einsum("sqhd,skhd->shqk", query, keys, preferred_element_type=jnp.float32) * scale
    length = query.shape[1]
    causal = jnp.arange(length)[:, None] >= jnp.arange(length)[None, :]
    same = segs[:, None, :, None] == segs[:, None, None, :]
    return jnp.where(causal[None, None] & same, scores, -jnp.inf)


def after(value, *earlier):
    return lax.optimization_barrier((value,) + earlier)[0]


def ring_place(position, count):
    position = position % count
    return jnp.where(position < count // 2, 2 * position, 2 * (count - 1 - position) + 1)


class Ring:
    def __init__(self, axis):
        self.axis = axis
        self.count = count = lax.axis_size(axis)
        order = [i for i in range(0, count, 2)] + [i for i in range(count - 1, 0, -2)]
        self.ahead = [(order[i], order[(i + 1) % count]) for i in range(count)]
        self.behind = [(b, a) for a, b in self.ahead]
        me = lax.axis_index(axis)
        self.position = jnp.where(me % 2 == 0, me // 2, count - 1 - me // 2)
        self.half = count // 2
        self.offsets = [0]
        for step in range(1, self.half):
            self.offsets += [-step, step]
        self.offsets.append(self.half)
        self.indices = [ring_place(self.position + o + count, count) for o in self.offsets]

    def gather(self, block):
        out = [block]
        fore = back = block
        for _ in range(1, self.half):
            fore = lax.ppermute(fore, self.axis, self.ahead)
            back = lax.ppermute(back, self.axis, self.behind)
            out += [fore, back]
        cut = block.shape[0] // 2
        first = lax.ppermute(fore[:cut], self.axis, self.ahead)
        second = lax.ppermute(back[cut:], self.axis, self.behind)
        out.append(jnp.concatenate([first, second], axis=0))
        return out

    def placed(self, blocks):
        whole = jnp.zeros((self.count,) + blocks[0].shape, blocks[0].dtype)
        for index, block in zip(self.indices, blocks):
            whole = lax.dynamic_update_slice(whole, block[None], (index,) + (0,) * block.ndim)
        return whole

    def scatter_sum(self, part):
        fp, low = jnp.float32, jnp.bfloat16
        far = part(self.count - 1)
        cut = far.shape[0] // 2
        fore = lax.ppermute(far[:cut].astype(low), self.axis, self.ahead).astype(fp)
        back = lax.ppermute(far[cut:].astype(low), self.axis, self.behind).astype(fp)
        for step in range(self.half - 1, 0, -1):
            mine_f = part(2 * step).astype(fp)
            mine_b = part(2 * step - 1).astype(fp)
            if step == self.half - 1:
                mine_f = jnp.concatenate([mine_f[:cut] + fore, mine_f[cut:]], axis=0)
                mine_b = jnp.concatenate([mine_b[:cut], mine_b[cut:] + back], axis=0)
            else:
                mine_f = mine_f + fore
                mine_b = mine_b + back
            fore = lax.ppermute(mine_f.astype(low), self.axis, self.ahead).astype(fp)
            back = lax.ppermute(mine_b.astype(low), self.axis, self.behind).astype(fp)
        own = part(0).astype(fp)
        if self.half == 1:
            return own + jnp.concatenate([fore, back], axis=0)
        return own + fore + back


def swap(value, axis, bit):
    count = lax.axis_size(axis)
    return lax.ppermute(value, axis, [(i, i ^ bit) for i in range(count)])


def bits_of(count):
    bits = []
    bit = count // 2
    while bit >= 1:
        bits.append(bit)
        bit //= 2
    return bits


def cube_gather(block, axis):
    out = [block]
    for bit in bits_of(lax.axis_size(axis)):
        out += [swap(b, axis, bit) for b in out]
    return out


def cube_order(count):
    order = [0]
    for bit in bits_of(count):
        order += [o ^ bit for o in order]
    return order


def cube_place(blocks, axis):
    me = lax.axis_index(axis)
    whole = jnp.zeros((len(blocks),) + blocks[0].shape, blocks[0].dtype)
    for o, block in zip(cube_order(len(blocks)), blocks):
        whole = lax.dynamic_update_slice(whole, block[None], (me ^ o,) + (0,) * block.ndim)
    return whole


def cube_scatter(parts, axis, near=jnp.bfloat16, far=jnp.bfloat16):
    fp = jnp.float32
    parts = list(parts)
    for bit in reversed(bits_of(lax.axis_size(axis))):
        half = len(parts) // 2
        kind = near if bit == 1 else far
        got = [swap(p.astype(kind), axis, bit).astype(fp) for p in parts[half:]]
        parts = [p.astype(fp) + g for p, g in zip(parts[:half], got)]
    return parts[0]


def per_device(
    block_in,
    cotangent,
    segments,
    expert_ids,
    attn_gain,
    w_query,
    w_key,
    w_value,
    query_gain,
    key_gain,
    w_out,
    ffn_gain,
    router,
    w_gate,
    w_up,
    w_down,
):
    fp = jnp.float32
    low = jnp.bfloat16
    ring = Ring("dp")
    n_data = lax.axis_size("dp")
    n_ten = lax.axis_size("tensor")
    me_t = lax.axis_index("tensor")
    rows_here, width = block_in.shape
    tok_rows = segments.shape[0]
    seqs = tok_rows // SEQ
    wide = w_query.shape[1]
    wrows = w_query.shape[0]
    experts = router.shape[1]
    local_exp = w_gate.shape[0]
    heads_here = query_gain.shape[0]
    head_size = wide // heads_here
    scale = head_size ** (-0.5)
    first_expert = lax.axis_index("dp") * local_exp
    order_t = cube_order(n_ten)

    def dot(a, b):
        return jnp.dot(a, b, preferred_element_type=fp)

    def dot_t(a, b):
        return lax.dot_general(a, b, (((1,), (1,)), ((), ())), preferred_element_type=fp)

    def dot_k(a, b):
        return lax.dot_general(a, b, (((0,), (0,)), ((), ())), preferred_element_type=fp)

    in_blocks = cube_gather(block_in, "tensor")
    in_all = cube_place(in_blocks, "tensor").reshape(tok_rows, width)

    sizes = [attn_gain.size, ffn_gain.size, query_gain.size, key_gain.size, router.size, expert_ids.size]
    flat = jnp.concatenate(
        [
            attn_gain,
            ffn_gain,
            query_gain.reshape(-1),
            key_gain.reshape(-1),
            router.reshape(-1),
            expert_ids.astype(low).reshape(-1),
        ]
    )
    small_rows = -(-flat.size // (2 * wide * 32)) * 32
    flat = jnp.pad(flat, (0, small_rows * 2 * wide - flat.size)).reshape(small_rows, 2 * wide)
    qk_blocks = ring.gather(
        jnp.concatenate([flat, jnp.concatenate([w_query, w_key], axis=1)], axis=0)
    )
    qk_cols = ring.placed([b[small_rows:] for b in qk_blocks]).reshape(width, 2 * wide)
    smalls = jnp.stack([b[:small_rows].reshape(-1) for b in qk_blocks])
    ids_rel = smalls[:, sum(sizes[:5]) : sum(sizes)].reshape(n_data * rows_here, -1).astype(jnp.int32)
    place = jnp.stack(ring.indices)
    in_order = (place[None, :] == jnp.arange(n_data)[:, None]).astype(low)
    smalls = jnp.dot(in_order, smalls[:, : sum(sizes[:5])], preferred_element_type=fp)
    cuts = [sum(sizes[:i]) for i in range(6)]
    gain_one, gain_two, q_gainf, k_gainf, route = [
        smalls[:, cuts[i] : cuts[i + 1]] for i in range(5)
    ]
    attn_g = gain_one.reshape(-1)
    ffn_g = gain_two.reshape(-1)

    def by_head(g):
        return g.reshape(n_data, heads_here, -1).transpose(1, 0, 2).reshape(-1)

    q_gainf = by_head(q_gainf)
    k_gainf = by_head(k_gainf)
    route_cols = route.astype(low).reshape(width, experts)

    v_blocks = ring.gather(after(w_value, qk_blocks[-1]))
    value_cols = ring.placed(v_blocks).reshape(width, wide)
    o_blocks = ring.gather(after(w_out, v_blocks[-1]))
    out_rows = ring.placed(o_blocks).transpose(1, 0, 2).reshape(wide, width)
    g_blocks = ring.gather(after(cotangent, o_blocks[-1]))

    last = in_blocks[-1]
    full = []
    for e in range(local_exp):
        got = []
        for w, axis in ((w_gate, 1), (w_up, 1), (w_down, 0)):
            blocks = cube_gather(after(w[e], last), "tensor")
            last = blocks[len(blocks) // 2 - 1]
            got.append(jnp.concatenate(blocks, axis=axis))
        full.append(got)

    all_full = in_all.astype(fp)
    r_all = rstd_of(all_full)
    n_all = all_full * r_all
    h_all = (n_all * attn_g).astype(low)
    qk_raw = dot(h_all, qk_cols)
    q_raw, k_raw = qk_raw[:, :wide], qk_raw[:, wide:]
    value = dot(h_all, value_cols).astype(low)
    squares = lax.psum(
        jnp.stack([jnp.sum(q_raw * q_raw, axis=-1), jnp.sum(k_raw * k_raw, axis=-1)]), "tensor"
    )
    r_q = lax.rsqrt(squares[0] / width + EPS)[:, None]
    r_k = lax.rsqrt(squares[1] / width + EPS)[:, None]
    cosine, sine = rope_tables(tok_rows, head_size)
    q_rot = rotate((q_raw * r_q * q_gainf).reshape(tok_rows, heads_here, head_size), cosine, sine)
    k_rot = rotate((k_raw * r_k * k_gainf).reshape(tok_rows, heads_here, head_size), cosine, sine)
    head_shape = (seqs, SEQ, heads_here, head_size)
    q_low = q_rot.astype(low).reshape(head_shape)
    k_low = k_rot.astype(low).reshape(head_shape)
    v_low = value.reshape(head_shape)
    seg_rows = segments.reshape(seqs, SEQ)
    masked = masked_scores(q_low, k_low, seg_rows, scale)
    top = jnp.max(masked, axis=-1, keepdims=True)
    lse = top + jnp.log(jnp.sum(jnp.exp(masked - top), axis=-1, keepdims=True))
    prob_low = jnp.exp(masked - lse).astype(low)
    heads_out = jnp.einsum("shqk,skhd->sqhd", prob_low, v_low, preferred_element_type=fp).astype(
        low
    )
    attn_heads = heads_out.reshape(tok_rows, -1)

    def token_block(values, o):
        return lax.dynamic_slice_in_dim(values, (me_t ^ o) * rows_here, rows_here, axis=0)

    out_parts = [dot(token_block(attn_heads, o), out_rows) for o in order_t]
    in_full = block_in.astype(fp)
    resid = in_full + cube_scatter(out_parts, "tensor", near=fp)
    r_two = rstd_of(resid)
    n_two = resid * r_two
    h_two = (n_two * ffn_g).astype(low)
    probs = jax.nn.softmax(dot(h_two, route_cols), axis=-1)

    h_blocks = ring.gather(after(h_two, g_blocks[-1]))
    groups = [(0, 3), (3, 5), (5, n_data)] if n_data == 8 else [(0, n_data)]
    acts, d_gates, d_ups, d_wts, y_parts, dh_parts, hs, gs = [], [], [], [], [], [], [], []
    for start, stop in groups:
        h_c = jnp.concatenate(h_blocks[start:stop], axis=0)
        g_c = jnp.concatenate(g_blocks[start:stop], axis=0)
        ids_c = ids_rel[start * rows_here : stop * rows_here]
        probs_c = jax.nn.softmax(dot(h_c, route_cols), axis=-1)
        y_c = dh_c = None
        act_e, dg_e, du_e, dw_e = [], [], [], []
        for e in range(local_exp):
            wg, wu, wd = full[e]
            number = first_expert + e
            chosen = jnp.any(ids_c == number, axis=1, keepdims=True)
            here = (jnp.arange(experts) == number)[None, :]
            weight = jnp.where(chosen, jnp.sum(jnp.where(here, probs_c, 0.0), axis=1, keepdims=True), 0.0)
            gate = dot(h_c, wg)
            up = dot(h_c, wu)
            back = dot_t(g_c, wd)
            sig = jax.nn.sigmoid(gate)
            act = gate * sig * up
            dw_e.append(jnp.where(chosen, jnp.sum(act * back, axis=1, keepdims=True), 0.0))
            d_act = back * weight
            act_e.append((act * weight).astype(low))
            dg_e.append((d_act * up * sig * (1.0 + gate * (1.0 - sig))).astype(low))
            du_e.append((d_act * gate * sig).astype(low))
            y_e = dot(act_e[e], wd)
            y_c = y_e if y_c is None else y_c + y_e
            dh_e = dot_t(dg_e[e], wg) + dot_t(du_e[e], wu)
            dh_c = dh_e if dh_c is None else dh_c + dh_e
        acts.append(act_e)
        d_gates.append(dg_e)
        d_ups.append(du_e)
        d_wts.append(dw_e)
        y_parts.append(y_c.astype(low))
        dh_parts.append(dh_c.astype(low))
        hs.append(h_c)
        gs.append(g_c)

    def block_of(parts, k):
        for (start, stop), part in zip(groups, parts):
            if start <= k < stop:
                return part[(k - start) * rows_here : (k - start + 1) * rows_here]

    extra = -(-2 * experts // 128) * 128
    wt_parts = []
    for dw_e in d_wts:
        exact = sum(
            jnp.where((jnp.arange(experts) == first_expert + e)[None, :], dw_e[e], 0.0)
            for e in range(local_exp)
        )
        top_part = exact.astype(low)
        rest = (exact - top_part.astype(fp)).astype(low)
        both = jnp.concatenate([top_part, rest], axis=1)
        wt_parts.append(jnp.pad(both, ((0, 0), (0, extra - 2 * experts))))

    sums = ring.scatter_sum(
        lambda k: jnp.concatenate([block_of(dh_parts, k), block_of(wt_parts, k)], axis=1)
    )
    d_h_moe = sums[:, :width]
    d_probs = sums[:, width : width + experts] + sums[:, width + experts : width + 2 * experts]

    h_cat = jnp.concatenate(hs, axis=0)
    g_cat = jnp.concatenate(gs, axis=0)
    piece = w_gate.shape[2]
    d_w_gate, d_w_up, d_w_down = [], [], []
    for e in range(local_exp):
        act_c = jnp.concatenate([a[e] for a in acts], axis=0)
        dg_c = jnp.concatenate([a[e] for a in d_gates], axis=0)
        du_c = jnp.concatenate([a[e] for a in d_ups], axis=0)
        gd = [dot_k(act_c[:, j * piece : (j + 1) * piece], g_cat) for j in range(n_ten)]
        d_w_down.append(cube_scatter([x.astype(low) for x in gd], "tensor"))
        gg = [dot_k(h_cat, dg_c[:, j * piece : (j + 1) * piece]) for j in range(n_ten)]
        d_w_gate.append(cube_scatter([x.astype(low) for x in gg], "tensor"))
        gu = [dot_k(h_cat, du_c[:, j * piece : (j + 1) * piece]) for j in range(n_ten)]
        d_w_up.append(cube_scatter([x.astype(low) for x in gu], "tensor"))
    d_w_gate, d_w_up, d_w_down = jnp.stack(d_w_gate), jnp.stack(d_w_up), jnp.stack(d_w_down)

    g_full = cotangent.astype(fp)
    d_logits = (probs * (d_probs - jnp.sum(probs * d_probs, axis=-1, keepdims=True))).astype(low)
    router_part = dot_k(d_logits, h_two)
    d_h_two = d_h_moe + dot_t(d_logits, route_cols)
    ffn_part = jnp.sum(d_h_two * n_two, axis=0)
    m_two = d_h_two * ffn_g
    d_resid = g_full + r_two * (m_two - n_two * jnp.mean(m_two * n_two, axis=-1, keepdims=True))
    carried = -(-(experts + 1) // 16) * 16
    with_sums = jnp.concatenate(
        [
            d_resid.astype(low),
            jnp.pad(
                jnp.concatenate([router_part, ffn_part[None]], axis=0),
                ((0, carried - experts - 1), (0, 0)),
            ).astype(low),
        ],
        axis=0,
    )
    res_blocks = cube_gather(with_sums, "tensor")
    d_resid_all = cube_place([b[:rows_here] for b in res_blocks], "tensor").reshape(tok_rows, width)
    small_sum = sum(b[rows_here:].astype(fp) for b in res_blocks)
    small_sum = small_sum.astype(low).reshape(carried, n_data, -1).transpose(1, 0, 2)

    wo_part = lax.dot_general(
        attn_heads,
        d_resid_all.reshape(tok_rows, n_data, -1),
        (((0,), (0,)), ((), ())),
        preferred_element_type=fp,
    ).astype(low).transpose(1, 0, 2)
    d_heads = dot_t(d_resid_all, out_rows).astype(low).reshape(head_shape)
    prob = jnp.exp(masked_scores(q_low, k_low, seg_rows, scale) - lse)
    d_value = jnp.einsum("shqk,sqhd->skhd", prob.astype(low), d_heads, preferred_element_type=fp)
    d_prob = jnp.einsum("sqhd,skhd->shqk", d_heads, v_low, preferred_element_type=fp)
    delta = jnp.sum(prob * d_prob, axis=-1, keepdims=True)
    d_score = (prob * (d_prob - delta) * scale).astype(low)
    d_q_rot = jnp.einsum("shqk,skhd->sqhd", d_score, k_low, preferred_element_type=fp)
    d_k_rot = jnp.einsum("shqk,sqhd->skhd", d_score, q_low, preferred_element_type=fp)
    d_q_norm = unrotate(d_q_rot.reshape(tok_rows, heads_here, head_size), cosine, sine).reshape(
        tok_rows, -1
    )
    d_k_norm = unrotate(d_k_rot.reshape(tok_rows, heads_here, head_size), cosine, sine).reshape(
        tok_rows, -1
    )
    qg_part = jnp.sum(d_q_norm * q_raw * r_q, axis=0)
    kg_part = jnp.sum(d_k_norm * k_raw * r_k, axis=0)
    u_q = d_q_norm * q_gainf
    u_k = d_k_norm * k_gainf
    inner = lax.psum(
        jnp.stack([jnp.sum(u_q * q_raw, axis=-1), jnp.sum(u_k * k_raw, axis=-1)]), "tensor"
    )
    d_q_raw = (r_q * u_q - q_raw * r_q**3 * (inner[0] / width)[:, None]).astype(low)
    d_k_raw = (r_k * u_k - k_raw * r_k**3 * (inner[1] / width)[:, None]).astype(low)
    d_value_low = d_value.reshape(tok_rows, -1).astype(low)

    o_sum = ring.scatter_sum(
        lambda k: jnp.concatenate(
            [
                lax.dynamic_index_in_dim(wo_part, ring.indices[k], 0, keepdims=False),
                lax.dynamic_index_in_dim(small_sum, ring.indices[k], 0, keepdims=False),
            ],
            axis=0,
        )
    )
    d_w_out = o_sum[:wide]
    mine = lax.dynamic_slice_in_dim(o_sum[wide:], me_t * (width // n_data // n_ten), width // n_data // n_ten, axis=1)
    d_router = mine[:experts].T
    d_ffn_gain = mine[experts]

    wv_part = dot_k(h_all, d_value_low).astype(low).reshape(n_data, wrows, wide)
    d_w_value = ring.scatter_sum(
        lambda k: lax.dynamic_index_in_dim(wv_part, ring.indices[k], 0, keepdims=False)
    )
    moe = ring.scatter_sum(lambda k: block_of(y_parts, k))
    block_out = (resid + moe).astype(low)

    d_qk = jnp.concatenate([d_q_raw, d_k_raw], axis=1)
    qk_part = dot_k(h_all, d_qk).astype(low).reshape(n_data, wrows, 2 * wide)
    total = dot_t(d_qk, qk_cols) + dot_t(d_value_low, value_cols)
    attn_part = jnp.sum(total * n_all, axis=0)

    def by_dp(part):
        return part.reshape(heads_here, n_data, -1).transpose(1, 0, 2).reshape(n_data, -1)

    tails = jnp.concatenate(
        [attn_part.reshape(n_data, -1), by_dp(qg_part), by_dp(kg_part)], axis=1
    ).astype(low)
    tails = jnp.pad(tails, ((0, 0), (0, 2 * wide - tails.shape[1])))
    tails = jnp.pad(tails[:, None, :], ((0, 0), (0, 31), (0, 0)))
    qk_sum = ring.scatter_sum(
        lambda k: jnp.concatenate(
            [
                lax.dynamic_index_in_dim(qk_part, ring.indices[k], 0, keepdims=False),
                lax.dynamic_index_in_dim(tails, ring.indices[k], 0, keepdims=False),
            ],
            axis=0,
        )
    )
    d_w_query = qk_sum[:wrows, :wide]
    d_w_key = qk_sum[:wrows, wide:]
    tail = qk_sum[wrows]
    n_g = width // n_data
    d_attn_gain = lax.psum_scatter(tail[:n_g], "tensor", scatter_dimension=0, tiled=True)
    n_q = query_gain.size
    d_query_gain = tail[n_g : n_g + n_q].reshape(query_gain.shape)
    d_key_gain = tail[n_g + n_q : n_g + 2 * n_q].reshape(key_gain.shape)

    d_h_one = cube_scatter([token_block(total.astype(low), o) for o in order_t], "tensor")
    r_one = rstd_of(in_full)
    n_one = in_full * r_one
    m_one = d_h_one * attn_g
    d_block_in = d_resid + r_one * (m_one - n_one * jnp.mean(m_one * n_one, axis=-1, keepdims=True))
    return (
        block_out,
        d_block_in,
        d_attn_gain,
        d_w_query,
        d_w_key,
        d_w_value,
        d_query_gain,
        d_key_gain,
        d_w_out,
        d_ffn_gain,
        d_router,
        d_w_gate,
        d_w_up,
        d_w_down,
    )


def solution(mesh):
    placed = (
        P(("dp", "tensor"), None),
        P(("dp", "tensor"), None),
        P("dp"),
        P(("dp", "tensor"), None),
        P("dp"),
        P("dp", "tensor"),
        P("dp", "tensor"),
        P("dp", "tensor"),
        P("tensor", "dp"),
        P("tensor", "dp"),
        P("tensor", "dp"),
        P("dp"),
        P("dp", None),
        P("dp", None, "tensor"),
        P("dp", None, "tensor"),
        P("dp", "tensor", None),
    )
    return jax.shard_map(
        per_device,
        mesh=mesh,
        in_specs=placed,
        out_specs=(
            P(("dp", "tensor"), None),
            P(("dp", "tensor"), None),
            P(("dp", "tensor")),
            P("dp", "tensor"),
            P("dp", "tensor"),
            P("dp", "tensor"),
            P("tensor", "dp"),
            P("tensor", "dp"),
            P("tensor", "dp"),
            P(("dp", "tensor")),
            P(("dp", "tensor"), None),
            P("dp", None, "tensor"),
            P("dp", None, "tensor"),
            P("dp", "tensor", None),
        ),
        check_vma=False,
    )
```
